256 devices in a mesh: ctx: 64 (over z, x, core), kvh: 4 (over y).
Axes of the slice: x: 4, y: 4, z: 8, core: 2. Of those that a mesh axis runs over, the one named last changes fastest.
Arguments:
- query_act: bfloat16 [16384, 8192], P(('ctx', 'kvh')), may hold values from -6 to 6
- key_act: bfloat16 [16384, 1024], P(('ctx', 'kvh')), may hold values from -6 to 6
- value_act: bfloat16 [16384, 1024], P(('ctx', 'kvh')), may hold values from -6 to 6
- grad_out: bfloat16 [16384, 8192], P(('ctx', 'kvh')), may hold values from -6 to 6
Outputs:
- attn_out: bfloat16 [16384, 8192], P(('ctx', 'kvh'))
- grad_query: bfloat16 [16384, 8192], P(('ctx', 'kvh'))
- grad_key: bfloat16 [16384, 1024], P(('ctx', 'kvh'))
- grad_value: bfloat16 [16384, 1024], P(('ctx', 'kvh'))
The draws below stay inside these ranges and needn't reach their ends.
All inputs are finite; a program needn't handle non-finite values.
Results may differ from the reference program's by a relative error of at most 0.014.
Values may be sent and summed in bfloat16 or wider, within the bound.
A program may use at most 128 MiB of HBM per device.

```python
import jax
import jax.numpy as jnp
from jax import lax

KVH = 8
QPK = 8
HD = 128
BLK = 256
SEQ = 16384
LEVELS = 6
N_CTX = 64


def draw_query_act(key, part):
    rows_total = BLK * N_CTX
    base = jax.random.normal(jax.random.fold_in(key, 11), (rows_total, KVH * QPK * HD), jnp.float32)
    return jnp.clip(base, -6.0, 6.0).astype(jnp.bfloat16)


def draw_key_act(key, part):
    rows_total = BLK * N_CTX
    base = jax.random.normal(jax.random.fold_in(key, 21), (rows_total, KVH * HD), jnp.float32)
    return jnp.clip(base, -6.0, 6.0).astype(jnp.bfloat16)


def steps_of(stream_key, shape, split, low, high):
    def one(dim, parts):
        steps = jax.random.uniform(jax.random.fold_in(jax.random.fold_in(stream_key, 6), dim), (parts,), jnp.float32, low / len(split), high / len(split))
        return jnp.repeat(jnp.exp(steps), shape[dim] // parts).reshape((-1,) + (1,) * (len(shape) - dim - 1))

    factor_of = one(*split[0])
    for cut in split[1:]:
        factor_of = factor_of * one(*cut)
    return factor_of


def scatter_about(own_key, dims, scale, most, cuts=(), dtype=jnp.bfloat16):
    factor_of = steps_of(own_key, dims, cuts, -0.22, 0.18) if cuts else 1.0
    drawn = jax.random.normal(own_key, dims, jnp.float32) * scale * factor_of
    return jnp.minimum(jnp.maximum(drawn, -most), most).astype(dtype)


def setup_inputs(seed: int = 0) -> dict:
    keys = jax.random.split(jax.random.key(seed), 5)
    query_act = draw_query_act(jax.random.fold_in(keys[4], 71), 0)
    key_act = draw_key_act(jax.random.fold_in(keys[4], 71), 0)
    value_act = scatter_about(keys[2], (SEQ, KVH * HD), 1.0, 6.0, ((0, 256),))
    grad_out = scatter_about(keys[3], (SEQ, KVH * QPK * HD), 1.0, 6.0, ((0, 256),))
    return dict(query_act=query_act, key_act=key_act, value_act=value_act, grad_out=grad_out)


masked_score = -1e30


def reference(query_act, key_act, value_act, grad_out):
    scale = HD ** -0.5
    queries = query_act.reshape(N_CTX, BLK, KVH, QPK, HD)
    key_rows = key_act.reshape(N_CTX, BLK, KVH, HD)
    value_rows = value_act.reshape(N_CTX, BLK, KVH, HD)
    grad_rows = grad_out.reshape(N_CTX, BLK, KVH, QPK, HD)
    position = jnp.arange(BLK)
    causal = (position[None, :] <= position[:, None])[None, None]

    def one_block(carry, block):
        key_grad_all, value_grad_all = carry
        q_block = queries[block].astype(jnp.float32)
        g_block = grad_rows[block].astype(jnp.float32)
        listing = [(block, causal)]
        for level in range(LEVELS):
            distance = 1 << level
            source = jnp.maximum(block - distance, 0).astype(jnp.int32)
            valid = jnp.broadcast_to(block >= distance, (1, 1, 1, 1))
            listing.append((source, valid))
        scores_all = []
        maxima = []
        sums = []
        outs_all = []
        for source, mask in listing:
            key_f = key_rows[source].astype(jnp.float32)
            val_f = value_rows[source].astype(jnp.float32)
            scores = jnp.einsum('tgrd,ugd->grtu', q_block, key_f) * scale
            scores = jnp.where(mask, scores, masked_score)
            level_max = jnp.max(scores, axis=3)
            expo = jnp.where(mask, jnp.exp(scores - level_max[..., None]), 0.0)
            level_sum = jnp.sum(expo, axis=3)
            weights = expo.astype(jnp.bfloat16).astype(jnp.float32)
            level_out = jnp.einsum('grtu,ugd->tgrd', weights, val_f)
            scores_all.append(scores)
            maxima.append(level_max)
            sums.append(level_sum)
            outs_all.append(level_out)
        top = maxima[0]
        for level_max in maxima[1:]:
            top = jnp.maximum(top, level_max)
        total = jnp.zeros_like(top)
        acc = jnp.zeros_like(outs_all[0])
        for level_max, level_sum, level_out in zip(maxima, sums, outs_all):
            factor = jnp.exp(level_max - top)
            total = total + factor * level_sum
            acc = acc + jnp.transpose(factor, (2, 0, 1))[..., None] * level_out
        logsum = top + jnp.log(total)
        out_block = (acc / jnp.transpose(total, (2, 0, 1))[..., None]).astype(jnp.bfloat16)
        delta = jnp.transpose(jnp.sum(g_block * out_block.astype(jnp.float32), axis=3), (1, 2, 0))
        grad_q = jnp.zeros_like(q_block)
        for (source, mask), scores in zip(listing, scores_all):
            key_f = key_rows[source].astype(jnp.float32)
            val_f = value_rows[source].astype(jnp.float32)
            probs = jnp.where(mask, jnp.exp(scores - logsum[..., None]), 0.0)
            probs_low = probs.astype(jnp.bfloat16).astype(jnp.float32)
            grad_val = jnp.einsum('grtu,tgrd->ugd', probs_low, g_block)
            grad_prob = jnp.einsum('tgrd,ugd->grtu', g_block, val_f)
            grad_scores = (probs * (grad_prob - delta[..., None])).astype(jnp.bfloat16).astype(jnp.float32)
            grad_q = grad_q + scale * jnp.einsum('grtu,ugd->tgrd', grad_scores, key_f)
            grad_k = scale * jnp.einsum('grtu,tgrd->ugd', grad_scores, q_block)
            key_grad_all = key_grad_all.at[source].add(grad_k)
            value_grad_all = value_grad_all.at[source].add(grad_val)
        return (key_grad_all, value_grad_all), (out_block, grad_q.astype(jnp.bfloat16))

    start = (jnp.zeros((N_CTX, BLK, KVH, HD), jnp.float32), jnp.zeros((N_CTX, BLK, KVH, HD), jnp.float32))
    (key_grad_all, value_grad_all), (out_blocks, grad_blocks) = lax.scan(one_block, start, jnp.arange(N_CTX).astype(jnp.int32))
    width = KVH * QPK * HD
    attn_out = out_blocks.reshape(N_CTX * BLK, width)
    grad_query = grad_blocks.reshape(N_CTX * BLK, width)
    grad_key = key_grad_all.astype(jnp.bfloat16).reshape(N_CTX * BLK, KVH * HD)
    grad_value = value_grad_all.astype(jnp.bfloat16).reshape(N_CTX * BLK, KVH * HD)
    return (attn_out, grad_query, grad_key, grad_value)
```

```python
import jax
import jax.numpy as jnp
from jax import lax
from jax.experimental import pallas as pl
from jax.experimental.pallas import tpu as pltpu
from jax.sharding import PartitionSpec as P

HD = 128
QPK = 8
BLK = 256
NL = 7
SCALE = HD**-0.5
C2 = SCALE * 1.4426950408889634
F32 = jnp.float32
BF = jnp.bfloat16
GRP = 2


def nt(a, b):
    return lax.dot_general(a, b, (((1,), (1,)), ((), ())), preferred_element_type=F32)


def nn(a, b):
    return lax.dot_general(a, b, (((1,), (0,)), ((), ())), preferred_element_type=F32)


def head(g, r, valid, q_ref, g_ref, kv, kt_ref, vt_ref, out_ref, gq_ref, s_scr, dp_scr, p_scr, ds_scr, gs_scr, qs_scr):
    col = pl.multiple_of((g * QPK + r) * HD, HD)
    row = pl.multiple_of(r * BLK, BLK)
    q = q_ref[:, pl.ds(col, HD)]
    go = g_ref[:, pl.ds(col, HD)]
    kc = slice(g * HD, (g + 1) * HD)
    vc = slice((GRP + g) * HD, (GRP + g + 1) * HD)
    top = None
    for j in range(NL):
        s = nt(kv[j][:, kc], q)
        dp_scr[j] = nt(kv[j][:, vc], go)
        if j == 0:
            u = lax.broadcasted_iota(jnp.int32, (BLK, BLK), 0)
            t = lax.broadcasted_iota(jnp.int32, (BLK, BLK), 1)
            s = jnp.where(u <= t, s, -1e30)
        s_scr[j] = s
        mj = jnp.max(s, axis=0, keepdims=True)
        top = mj if j == 0 else jnp.maximum(top, jnp.where(valid[j], mj, -1e30))
    total = jnp.zeros((1, BLK), F32)
    acc = jnp.zeros((HD, BLK), F32)
    for j in range(NL):
        sub = top if j == 0 else jnp.where(valid[j], top, 1e30)
        p = jnp.exp2((s_scr[j] - sub) * C2)
        s_scr[j] = p
        total = total + jnp.sum(p, axis=0, keepdims=True)
        pb = p.astype(BF)
        p_scr[j, :, pl.ds(row, BLK)] = pb
        acc = acc + nn(vt_ref[j, g], pb)
    inv = 1.0 / total
    ot = (acc * inv).astype(BF)
    out_ref[:, pl.ds(col, HD)] = ot.T
    delta = jnp.sum(ot.astype(F32) * go.T.astype(F32), axis=0, keepdims=True)
    acc = jnp.zeros((HD, BLK), F32)
    for j in range(NL):
        ds = (s_scr[j] * (dp_scr[j] - delta)).astype(BF)
        ds_scr[j, :, pl.ds(row, BLK)] = ds
        acc = acc + nn(kt_ref[j, g], ds)
    gq_ref[:, pl.ds(col, HD)] = (acc * (inv * SCALE)).astype(BF).T
    invb = jnp.broadcast_to(inv, (HD, BLK)).T
    gs_scr[pl.ds(row, BLK), :] = (go.astype(F32) * invb).astype(BF)
    qs_scr[pl.ds(row, BLK), :] = (q.astype(F32) * (invb * SCALE)).astype(BF)


def kernel(*refs):
    q_ref, g_ref = refs[:2]
    kv = refs[2 : 2 + NL]
    out_ref, gq_ref = refs[9:11]
    gkv = refs[11 : 11 + NL]
    kt_ref, vt_ref, s_scr, dp_scr, p_scr, ds_scr, gs_scr, qs_scr = refs[18:]
    ctx = lax.axis_index("ctx")
    valid = [None] + [ctx >= 1 << j for j in range(NL - 1)]
    for g in range(GRP):
        kc = slice(g * HD, (g + 1) * HD)
        vc = slice((GRP + g) * HD, (GRP + g + 1) * HD)
        for j in range(NL):
            kt_ref[j, g] = kv[j][:, kc].T
            vt_ref[j, g] = kv[j][:, vc].T

        def body(r, _):
            head(g, r, valid, q_ref, g_ref, kv, kt_ref, vt_ref, out_ref, gq_ref, s_scr, dp_scr, p_scr, ds_scr, gs_scr, qs_scr)
            return 0

        lax.fori_loop(0, QPK, body, 0)
        for j in range(NL):
            gkv[j][:, vc] = nn(p_scr[j], gs_scr[...]).astype(BF)
            gkv[j][:, kc] = nn(ds_scr[j], qs_scr[...]).astype(BF)


VM = pl.BlockSpec(memory_space=pltpu.VMEM)


def shifted(array, by):
    peers = lax.axis_size("ctx")
    return lax.ppermute(array, "ctx", [(i, i + by) for i in range(peers) if 0 <= i + by < peers])


def a2a_in(x):
    return lax.all_to_all(x, "kvh", split_axis=1, concat_axis=0, tiled=True)


def a2a_out(x):
    return lax.all_to_all(x, "kvh", split_axis=0, concat_axis=1, tiled=True)


def shards(query_act, key_act, value_act, grad_out):
    tok = query_act.shape[0]
    kv_loc = jnp.concatenate([key_act.reshape(tok, 4, -1), value_act.reshape(tok, 4, -1)], 2).reshape(tok, -1)
    own = a2a_in(kv_loc)
    kv = [own] + [shifted(own, 1 << j) for j in range(NL - 1)]
    q = a2a_in(query_act)
    go = a2a_in(grad_out)
    res = pl.pallas_call(
        kernel,
        out_shape=(jax.ShapeDtypeStruct((BLK, GRP * QPK * HD), BF),) * 2
        + (jax.ShapeDtypeStruct((BLK, 2 * GRP * HD), BF),) * NL,
        in_specs=[VM] * (2 + NL),
        out_specs=(VM,) * (2 + NL),
        scratch_shapes=[pltpu.VMEM((NL, GRP, HD, BLK), BF)] * 2
        + [pltpu.VMEM((NL, BLK, BLK), F32)] * 2
        + [pltpu.VMEM((NL, BLK, QPK * BLK), BF)] * 2
        + [pltpu.VMEM((QPK * BLK, HD), BF)] * 2,
        compiler_params=pltpu.CompilerParams(vmem_limit_bytes=56 * 2**20),
    )(q, go, *kv)
    out, gq = res[:2]
    gkv = res[2:]
    total = gkv[0].astype(F32)
    for j in range(NL - 1):
        total = total + shifted(gkv[1 + j], -(1 << j)).astype(F32)
    back = a2a_out(total.astype(BF)).reshape(tok, 4, 2, -1)
    return (
        a2a_out(out),
        a2a_out(gq),
        back[:, :, 0].reshape(tok, -1),
        back[:, :, 1].reshape(tok, -1),
    )


def solution(mesh):
    spec = P(("ctx", "kvh"), None)
    return jax.shard_map(shards, mesh=mesh, in_specs=(spec,) * 4, out_specs=(spec,) * 4, check_vma=False)
```

```python
import jax
import jax.numpy as jnp
from jax import lax
from jax.experimental import pallas as pl
from jax.experimental.pallas import tpu as pltpu
from jax.sharding import PartitionSpec as P

HD = 128
QPK = 8
BLK = 256
NL = 7
GRP = 2
NKV = 4
NCTX = 64
TOK = BLK // NKV
CH = 2
NCH = GRP * QPK // CH
CW = CH * HD
QW = GRP * QPK * HD
KW = GRP * HD
SCALE = HD**-0.5
C2 = SCALE * 1.4426950408889634
F32 = jnp.float32
BF = jnp.bfloat16
MESH = pl.DeviceIdType.MESH
ctx_offsets = (1, 2, 4, 6, 7, 8, 16, 32, 48, 56, 57, 58, 60, 62, 63)


def nt(a, b):
    return lax.dot_general(a, b, (((1,), (1,)), ((), ())), preferred_element_type=F32)


def nn(a, b):
    return lax.dot_general(a, b, (((1,), (0,)), ((), ())), preferred_element_type=F32)


def head(g, r, valid, qbuf, gbuf, kvb, ktb, vtb, outb, gqb, s_scr, dp_scr, p_scr, ds_scr, gs_scr, qs_scr):
    col = pl.multiple_of((g * QPK + r) * HD, HD)
    row = pl.multiple_of(r * BLK, BLK)
    q = qbuf[:, pl.ds(col, HD)]
    go = gbuf[:, pl.ds(col, HD)]
    top = None
    for j in range(NL):
        s = nt(kvb[g, j, :, :HD], q)
        dp_scr[j] = nt(kvb[g, j, :, HD:], go)
        if j == 0:
            u = lax.broadcasted_iota(jnp.int32, (BLK, BLK), 0)
            t = lax.broadcasted_iota(jnp.int32, (BLK, BLK), 1)
            s = jnp.where(u <= t, s, -1e30)
        s_scr[j] = s
        mj = jnp.max(s, axis=0, keepdims=True)
        top = mj if j == 0 else jnp.maximum(top, jnp.where(valid[j], mj, -1e30))
    total = jnp.zeros((1, BLK), F32)
    acc = jnp.zeros((HD, BLK), F32)
    for j in range(NL):
        sub = top if j == 0 else jnp.where(valid[j], top, 1e30)
        p = jnp.exp2((s_scr[j] - sub) * C2)
        s_scr[j] = p
        total = total + jnp.sum(p, axis=0, keepdims=True)
        pb = p.astype(BF)
        p_scr[j, :, pl.ds(row, BLK)] = pb
        acc = acc + nn(vtb[g, j], pb)
    inv = 1.0 / total
    ot = (acc * inv).astype(BF)
    outb[:, pl.ds(col, HD)] = ot.T
    delta = jnp.sum(ot.astype(F32) * go.T.astype(F32), axis=0, keepdims=True)
    acc = jnp.zeros((HD, BLK), F32)
    for j in range(NL):
        ds = (s_scr[j] * (dp_scr[j] - delta)).astype(BF)
        ds_scr[j, :, pl.ds(row, BLK)] = ds
        acc = acc + nn(ktb[g, j], ds)
    gqb[:, pl.ds(col, HD)] = (acc * (inv * SCALE)).astype(BF).T
    invb = jnp.broadcast_to(inv, (HD, BLK)).T
    gs_scr[pl.ds(row, BLK), :] = (go.astype(F32) * invb).astype(BF)
    qs_scr[pl.ds(row, BLK), :] = (q.astype(F32) * (invb * SCALE)).astype(BF)


def kernel(
    q_in, k_in, v_in, g_in,
    out_o, gq_o, gk_o, gv_o,
    qbuf, gbuf, kvb, ktb, vtb, outb, gqb,
    s_scr, dp_scr, p_scr, ds_scr, gs_scr, qs_scr,
    gsend, grecv, own, part8, gfin,
    loc_sem, in_ss, in_rs, kv_ss, kv_rs, ring_ss, ring_rs, gr_ss, gr_rs, out_ss, out_rs, out_loc, fin_ss, fin_rs, fin_loc,
):
    c = lax.axis_index("ctx")
    h = lax.axis_index("kvh")
    low = lax.rem(c, 8)
    valid = [None] + [c >= 1 << j for j in range(NL - 1)]
    mine = pl.ds(pl.multiple_of(h * TOK, TOK), TOK)

    local = [
        pltpu.make_async_copy(q_in.at[:, pl.ds(pl.multiple_of(h * QW, QW), QW)], qbuf.at[mine], loc_sem.at[0]),
        pltpu.make_async_copy(g_in.at[:, pl.ds(pl.multiple_of(h * QW, QW), QW)], gbuf.at[mine], loc_sem.at[1]),
    ]
    for g in range(GRP):
        src = pl.ds(pl.multiple_of(h * KW + g * HD, HD), HD)
        local.append(pltpu.make_async_copy(k_in.at[:, src], kvb.at[g, 0, mine, pl.ds(0, HD)], loc_sem.at[2 + 2 * g]))
        local.append(pltpu.make_async_copy(v_in.at[:, src], kvb.at[g, 0, mine, pl.ds(HD, HD)], loc_sem.at[3 + 2 * g]))
    for cp in local:
        cp.start()
    for j in range(1, NL):
        @pl.when(jnp.logical_not(valid[j]))
        def _():
            for g in range(GRP):
                kvb[g, j] = jnp.zeros((BLK, 2 * HD), BF)

    bar = pltpu.get_barrier_semaphore()
    for o in range(1, NKV):
        pl.semaphore_signal(bar, 1, device_id={"kvh": lax.rem(h + o, NKV)}, device_id_type=MESH)
    for o in ctx_offsets:
        pl.semaphore_signal(bar, 1, device_id={"ctx": lax.rem(c + o, NCTX)}, device_id_type=MESH)
    pl.semaphore_wait(bar, NKV - 1 + len(ctx_offsets))

    def kv_copy(g, a, o):
        p = lax.rem(h + o, NKV)
        ref = (k_in, v_in)[a]
        return pltpu.make_async_remote_copy(
            ref.at[:, pl.ds(pl.multiple_of(p * KW + g * HD, HD), HD)],
            kvb.at[g, 0, mine, pl.ds(a * HD, HD)],
            kv_ss.at[g, a, o - 1], kv_rs.at[g, a, o - 1],
            device_id={"kvh": p}, device_id_type=MESH,
        )

    def in_copy(k, a, o):
        p = lax.rem(h + o, NKV)
        ref, buf = ((q_in, qbuf), (g_in, gbuf))[a]
        return pltpu.make_async_remote_copy(
            ref.at[:, pl.ds(pl.multiple_of(p * QW + k * CW, CW), CW)],
            buf.at[mine, pl.ds(pl.multiple_of(k * CW, CW), CW)],
            in_ss.at[k, a, o - 1], in_rs.at[k, a, o - 1],
            device_id={"kvh": p}, device_id_type=MESH,
        )

    def out_copy(k, a, o):
        p = lax.rem(h + o, NKV)
        buf, ref = ((outb, out_o), (gqb, gq_o))[a]
        return pltpu.make_async_remote_copy(
            buf.at[pl.ds(pl.multiple_of(p * TOK, TOK), TOK), pl.ds(pl.multiple_of(k * CW, CW), CW)],
            ref.at[:, pl.ds(pl.multiple_of(h * QW + k * CW, CW), CW)],
            out_ss.at[k, a, o - 1], out_rs.at[k, a, o - 1],
            device_id={"kvh": p}, device_id_type=MESH,
        )

    def out_local(k, a):
        buf, ref = ((outb, out_o), (gqb, gq_o))[a]
        return pltpu.make_async_copy(
            buf.at[mine, pl.ds(pl.multiple_of(k * CW, CW), CW)],
            ref.at[:, pl.ds(pl.multiple_of(h * QW + k * CW, CW), CW)],
            out_loc.at[k, a],
        )

    def fin_copy(g, a, o):
        p = lax.rem(h + o, NKV)
        return pltpu.make_async_remote_copy(
            gfin.at[g, pl.ds(pl.multiple_of(p * TOK, TOK), TOK), pl.ds(a * HD, HD)],
            (gk_o, gv_o)[a].at[:, pl.ds(pl.multiple_of(h * KW + g * HD, HD), HD)],
            fin_ss.at[g, a, o - 1], fin_rs.at[g, a, o - 1],
            device_id={"kvh": p}, device_id_type=MESH,
        )

    def fin_local(g, a):
        return pltpu.make_async_copy(
            gfin.at[g, mine, pl.ds(a * HD, HD)],
            (gk_o, gv_o)[a].at[:, pl.ds(pl.multiple_of(h * KW + g * HD, HD), HD)],
            fin_loc.at[g, a],
        )

    def ring(g, j, from8):
        src, at = (4, c - 8) if from8 else (0, c)
        return pltpu.make_async_remote_copy(
            kvb.at[g, src], kvb.at[g, j], ring_ss.at[g, j], ring_rs.at[g, j],
            device_id={"ctx": at + (1 << (j - 1))}, device_id_type=MESH,
        )

    def send_own(g):
        for j in (4, 2, 6, 3, 1):
            d = 1 << (j - 1)
            cond = c + d < NCTX if j >= 4 else low + d < 8

            @pl.when(cond)
            def _():
                ring(g, j, False).start()

    def forward(g):
        @pl.when(c >= 8)
        def _():
            ring(g, 4, False).wait_recv()
            for j in (5, 2, 3, 1):
                d = 1 << (j - 1)

                @pl.when(c + 8 < NCTX if j == 5 else low + d >= 8)
                def _():
                    ring(g, j, True).start()

    def term(g, j):
        d = 1 << (j - 1)
        if j in (4, 6):
            dest = c - d
        elif j == 5:
            dest = c - 8
        else:
            dest = jnp.where(low >= d, c - d, c - d + 8)
        return pltpu.make_async_remote_copy(
            gsend.at[g, j], grecv.at[g, j], gr_ss.at[g, j], gr_rs.at[g, j],
            device_id={"ctx": dest}, device_id_type=MESH,
        )

    for g in range(GRP):
        for o in (1, 3, 2):
            for a in range(2):
                kv_copy(g, a, o).start()

    def send_in(k, _):
        for a in range(2):
            for o in (1, 3, 2):
                in_copy(k, a, o).start()
        return 0

    lax.fori_loop(0, NCH, send_in, 0)
    for cp in local[2:]:
        cp.wait()
    for g in range(GRP):
        for o in (1, 3, 2):
            for a in range(2):
                kv_copy(g, a, o).wait_recv()
        send_own(g)
    for g in range(GRP):
        forward(g)
    for cp in local[:2]:
        cp.wait()

    def relay(g):
        t8 = part8[g]
        pick = [(5, jnp.logical_and(c >= 8, c + 8 < NCTX))]
        for j in (1, 2, 3):
            pick.append((j, jnp.logical_and(c >= 8, low + (1 << (j - 1)) >= 8)))
        part8[g] = t8
        for j, cond in pick:
            @pl.when(cond)
            def _():
                term(g, j).wait_recv()
                part8[g] = part8[g] + grecv[g, j].astype(F32)
        gsend[g, 4] = part8[g].astype(BF)

        @pl.when(c >= 8)
        def _():
            term(g, 4).start()

    def finish(g):
        pick = [(6, c + 32 < NCTX), (4, c + 8 < NCTX)]
        for j in (1, 2, 3):
            pick.append((j, low + (1 << (j - 1)) < 8))
        for j, cond in pick:
            @pl.when(cond)
            def _():
                term(g, j).wait_recv()
                own[g] = own[g] + grecv[g, j].astype(F32)
        gfin[g] = own[g].astype(BF)
        for a in range(2):
            for o in (1, 3, 2):
                fin_copy(g, a, o).start()
            fin_local(g, a).start()

    def group(g, _):
        for j in (1, 2, 3, 5, 6):
            @pl.when(valid[j])
            def _():
                ring(g, j, False).wait_recv()
        for j in range(NL):
            ktb[g, j] = kvb[g, j, :, :HD].T
            vtb[g, j] = kvb[g, j, :, HD:].T

        def body(r, _):
            k = g * (QPK // CH) + r // CH

            @pl.when(lax.rem(r, CH) == 0)
            def _():
                for a in range(2):
                    for o in range(1, NKV):
                        in_copy(k, a, o).wait_recv()

            head(g, r, valid, qbuf, gbuf, kvb, ktb, vtb, outb, gqb, s_scr, dp_scr, p_scr, ds_scr, gs_scr, qs_scr)

            @pl.when(lax.rem(r, CH) == CH - 1)
            def _():
                for a in range(2):
                    for o in (1, 3, 2):
                        out_copy(k, a, o).start()
                    out_local(k, a).start()

            @pl.when(jnp.logical_and(g == 1, r == 1))
            def _():
                relay(0)

            @pl.when(jnp.logical_and(g == 1, r == 4))
            def _():
                finish(0)

            return 0

        lax.fori_loop(0, QPK, body, 0)
        for j in (5, 3, 2, 1, 6, 4, 0):
            gk = nn(ds_scr[j], qs_scr[...])
            gv = nn(p_scr[j], gs_scr[...])
            if j in (0, 4):
                acc = own if j == 0 else part8
                acc[g, :, :HD] = gk
                acc[g, :, HD:] = gv
            else:
                gsend[g, j, :, :HD] = gk.astype(BF)
                gsend[g, j, :, HD:] = gv.astype(BF)

                @pl.when(valid[j])
                def _():
                    term(g, j).start()

        return 0

    lax.fori_loop(0, GRP, group, 0)
    relay(1)
    finish(1)

    def drain(k, _):
        for a in range(2):
            for o in range(1, NKV):
                in_copy(k, a, o).wait_send()
                out_copy(k, a, o).wait()
            out_local(k, a).wait()
        return 0

    lax.fori_loop(0, NCH, drain, 0)
    for g in range(GRP):
        for a in range(2):
            for o in range(1, NKV):
                kv_copy(g, a, o).wait_send()
                fin_copy(g, a, o).wait()
            fin_local(g, a).wait()
        for j in range(1, NL):
            d = 1 << (j - 1)
            if j in (4, 6):
                cond = c + d < NCTX
            elif j == 5:
                cond = jnp.logical_and(c >= 8, c + 8 < NCTX)
            else:
                cond = jnp.logical_or(low + d < 8, c >= 8)

            @pl.when(cond)
            def _():
                ring(g, j, False).wait_send()

            @pl.when(valid[j])
            def _():
                term(g, j).wait_send()


def shards(query_act, key_act, value_act, grad_out):
    hbm = pl.BlockSpec(memory_space=pl.ANY)
    dma = pltpu.SemaphoreType.DMA
    return tuple(
        pl.pallas_call(
            kernel,
            out_shape=tuple(jax.ShapeDtypeStruct(a.shape, BF) for a in (query_act, query_act, key_act, value_act)),
            in_specs=[hbm] * 4,
            out_specs=(hbm,) * 4,
            scratch_shapes=[pltpu.VMEM((BLK, QW), BF)] * 2
            + [pltpu.VMEM((GRP, NL, BLK, 2 * HD), BF)]
            + [pltpu.VMEM((GRP, NL, HD, BLK), BF)] * 2
            + [pltpu.VMEM((BLK, QW), BF)] * 2
            + [pltpu.VMEM((NL, BLK, BLK), F32)] * 2
            + [pltpu.VMEM((NL, BLK, QPK * BLK), BF)] * 2
            + [pltpu.VMEM((QPK * BLK, HD), BF)] * 2
            + [pltpu.VMEM((GRP, NL, BLK, 2 * HD), BF)] * 2
            + [pltpu.VMEM((GRP, BLK, 2 * HD), F32)] * 2
            + [pltpu.VMEM((GRP, BLK, 2 * HD), BF)]
            + [dma((6,))]
            + [dma((NCH, 2, 3))] * 2
            + [dma((GRP, 2, 3))] * 2
            + [dma((GRP, NL))] * 4
            + [dma((NCH, 2, 3))] * 2
            + [dma((NCH, 2))]
            + [dma((GRP, 2, 3))] * 2
            + [dma((GRP, 2))],
            compiler_params=pltpu.CompilerParams(
                vmem_limit_bytes=60 * 2**20, collective_id=0, has_side_effects=True
            ),
        )(query_act, key_act, value_act, grad_out)
    )


def solution(mesh):
    spec = P(("ctx", "kvh"), None)
    return jax.shard_map(shards, mesh=mesh, in_specs=(spec,) * 4, out_specs=(spec,) * 4, check_vma=False)
```

```python
import jax
import jax.numpy as jnp
from jax import lax
from jax.experimental import pallas as pl
from jax.experimental.pallas import tpu as pltpu
from jax.sharding import PartitionSpec as P

HD = 128
QPK = 8
BLK = 256
NL = 7
GRP = 2
NKV = 4
NCTX = 64
TOK = BLK // NKV
CH = 4
NSP = 4
NCH = GRP * QPK // CH
CW = CH * HD
QW = GRP * QPK * HD
KW = GRP * HD
SCALE = HD**-0.5
C2 = SCALE * 1.4426950408889634
F32 = jnp.float32
BF = jnp.bfloat16
MESH = pl.DeviceIdType.MESH
ctx_offsets = (1, 2, 4, 6, 7, 8, 16, 32, 48, 56, 57, 58, 60, 62, 63)


def nt(a, b):
    return lax.dot_general(a, b, (((1,), (1,)), ((), ())), preferred_element_type=F32)


def nn(a, b):
    return lax.dot_general(a, b, (((1,), (0,)), ((), ())), preferred_element_type=F32)


def head(g, r, valid, qbuf, gbuf, kvb, vtb, outb, s_scr, p_scr, ds_scr, gs_scr, qs_scr, st):
    col = pl.multiple_of((g * QPK + r) * HD, HD)
    row = pl.multiple_of(r * BLK, BLK)
    q = qbuf[:, pl.ds(col, HD)]
    go = gbuf[:, pl.ds(col, HD)]
    top = None
    for j in range(NL):
        s = nt(kvb[g, j, 0], q)
        if j == 0:
            u = lax.broadcasted_iota(jnp.int32, (BLK, BLK), 0)
            t = lax.broadcasted_iota(jnp.int32, (BLK, BLK), 1)
            s = jnp.where(u <= t, s, -1e30)
        s_scr[j] = s
        mj = jnp.max(s.reshape(BLK // 8, 8, BLK), axis=0)
        top = mj if j == 0 else jnp.maximum(top, jnp.where(valid[j], mj, -1e30))
    top = jnp.max(top, axis=0, keepdims=True)
    total = jnp.zeros((8, BLK), F32)
    acc = jnp.zeros((HD, BLK), F32)
    for j in range(NL):
        sub = top if j == 0 else jnp.where(valid[j], top, 1e30)
        p = jnp.exp2((s_scr[j] - sub) * C2)
        total = total + jnp.sum(p.reshape(BLK // 8, 8, BLK), axis=0)
        pb = p.astype(BF)
        p_scr[j, :, pl.ds(row, BLK)] = pb
        acc = acc + nn(vtb[g, j], pb)
    inv = 1.0 / jnp.sum(total, axis=0, keepdims=True)
    ot = (acc * inv).astype(BF)
    outb[:, pl.ds(col, HD)] = ot.T
    delta = jnp.sum(ot.astype(F32) * go.T.astype(F32), axis=0, keepdims=True)
    for j in range(NL):
        dp = nt(kvb[g, j, 1], go) - delta
        ds = (p_scr[j, :, pl.ds(row, BLK)].astype(F32) * dp).astype(BF)
        ds_scr[j, :, pl.ds(row, BLK)] = ds
    st[pl.ds(r, 1)] = inv * SCALE
    invb = jnp.broadcast_to(inv, (HD, BLK)).T
    gs_scr[pl.ds(row, BLK), :] = (go.astype(F32) * invb).astype(BF)
    qs_scr[pl.ds(row, BLK), :] = (q.astype(F32) * (invb * SCALE)).astype(BF)


def query_grad(g, r, ktb, gqb, ds_scr, st):
    col = pl.multiple_of((g * QPK + r) * HD, HD)
    row = pl.multiple_of(r * BLK, BLK)
    acc = jnp.zeros((HD, BLK), F32)
    for j in range(NL):
        acc = acc + nn(ktb[g, j], ds_scr[j, :, pl.ds(row, BLK)])
    gqb[:, pl.ds(col, HD)] = (acc * st[pl.ds(r, 1)]).astype(BF).T


def kernel(
    q_in, k_in, v_in, g_in,
    out_o, gq_o, gk_o, gv_o,
    qbuf, gbuf, kvb, ktb, vtb, outb, gqb,
    s_scr, p_scr, ds_scr, gs_scr, qs_scr, st,
    gsend, grecv, own, part8, gfin,
    loc_sem, in_ss, in_rs, kv_ss, kv_rs, ring_ss, ring_rs, gr_ss, gr_rs, out_ss, out_rs, out_loc, fin_ss, fin_rs, fin_loc,
):
    c = lax.axis_index("ctx")
    h = lax.axis_index("kvh")
    low = lax.rem(c, 8)
    valid = [None] + [c >= 1 << j for j in range(NL - 1)]
    mine = pl.ds(pl.multiple_of(h * TOK, TOK), TOK)

    local = [
        pltpu.make_async_copy(q_in.at[:, pl.ds(pl.multiple_of(h * QW, QW), QW)], qbuf.at[mine], loc_sem.at[0]),
        pltpu.make_async_copy(g_in.at[:, pl.ds(pl.multiple_of(h * QW, QW), QW)], gbuf.at[mine], loc_sem.at[1]),
    ]
    for g in range(GRP):
        src = pl.ds(pl.multiple_of(h * KW + g * HD, HD), HD)
        local.append(pltpu.make_async_copy(k_in.at[:, src], kvb.at[g, 0, 0, mine], loc_sem.at[2 + 2 * g]))
        local.append(pltpu.make_async_copy(v_in.at[:, src], kvb.at[g, 0, 1, mine], loc_sem.at[3 + 2 * g]))
    for cp in local:
        cp.start()
    for j in range(1, NL):
        @pl.when(jnp.logical_not(valid[j]))
        def _():
            for g in range(GRP):
                kvb[g, j] = jnp.zeros((2, BLK, HD), BF)

    bar = pltpu.get_barrier_semaphore()
    for o in range(1, NKV):
        pl.semaphore_signal(bar, 1, device_id={"kvh": lax.rem(h + o, NKV)}, device_id_type=MESH)
    for o in ctx_offsets:
        pl.semaphore_signal(bar, 1, device_id={"ctx": lax.rem(c + o, NCTX)}, device_id_type=MESH)
    pl.semaphore_wait(bar, NKV - 1 + len(ctx_offsets))

    def kv_copy(g, a, o):
        p = lax.rem(h + o, NKV)
        ref = (k_in, v_in)[a]
        return pltpu.make_async_remote_copy(
            ref.at[:, pl.ds(pl.multiple_of(p * KW + g * HD, HD), HD)],
            kvb.at[g, 0, a, mine],
            kv_ss.at[g, a, o - 1], kv_rs.at[g, a, o - 1],
            device_id={"kvh": p}, device_id_type=MESH,
        )

    def in_copy(k, a, o):
        p = lax.rem(h + o, NKV)
        ref, buf = ((q_in, qbuf), (g_in, gbuf))[a]
        return pltpu.make_async_remote_copy(
            ref.at[:, pl.ds(pl.multiple_of(p * QW + k * CW, CW), CW)],
            buf.at[mine, pl.ds(pl.multiple_of(k * CW, CW), CW)],
            in_ss.at[k, a, o - 1], in_rs.at[k, a, o - 1],
            device_id={"kvh": p}, device_id_type=MESH,
        )

    def out_copy(k, a, o):
        p = lax.rem(h + o, NKV)
        buf, ref = ((outb, out_o), (gqb, gq_o))[a]
        return pltpu.make_async_remote_copy(
            buf.at[pl.ds(pl.multiple_of(p * TOK, TOK), TOK), pl.ds(pl.multiple_of(k * CW, CW), CW)],
            ref.at[:, pl.ds(pl.multiple_of(h * QW + k * CW, CW), CW)],
            out_ss.at[k, a, o - 1], out_rs.at[k, a, o - 1],
            device_id={"kvh": p}, device_id_type=MESH,
        )

    def out_local(k, a):
        buf, ref = ((outb, out_o), (gqb, gq_o))[a]
        return pltpu.make_async_copy(
            buf.at[mine, pl.ds(pl.multiple_of(k * CW, CW), CW)],
            ref.at[:, pl.ds(pl.multiple_of(h * QW + k * CW, CW), CW)],
            out_loc.at[k, a],
        )

    def fin_copy(g, a, o):
        p = lax.rem(h + o, NKV)
        return pltpu.make_async_remote_copy(
            gfin.at[g, a, pl.ds(pl.multiple_of(p * TOK, TOK), TOK)],
            (gk_o, gv_o)[a].at[:, pl.ds(pl.multiple_of(h * KW + g * HD, HD), HD)],
            fin_ss.at[g, a, o - 1], fin_rs.at[g, a, o - 1],
            device_id={"kvh": p}, device_id_type=MESH,
        )

    def fin_local(g, a):
        return pltpu.make_async_copy(
            gfin.at[g, a, mine],
            (gk_o, gv_o)[a].at[:, pl.ds(pl.multiple_of(h * KW + g * HD, HD), HD)],
            fin_loc.at[g, a],
        )

    def ring(g, j, a, from8):
        src, at = (4, c - 8) if from8 else (0, c)
        return pltpu.make_async_remote_copy(
            kvb.at[g, src, a], kvb.at[g, j, a], ring_ss.at[g, j, a], ring_rs.at[g, j, a],
            device_id={"ctx": at + (1 << (j - 1))}, device_id_type=MESH,
        )

    def send_own(g):
        for a in range(2):
            for o in (1, 3, 2):
                kv_copy(g, a, o).wait_recv()
            for j in (4, 2, 6, 3, 1):
                d = 1 << (j - 1)

                @pl.when(c + d < NCTX if j >= 4 else low + d < 8)
                def _():
                    ring(g, j, a, False).start()

    def forward(g):
        @pl.when(c >= 8)
        def _():
            for a in range(2):
                ring(g, 4, a, False).wait_recv()
                for j in (5, 2, 3, 1):
                    d = 1 << (j - 1)

                    @pl.when(c + 8 < NCTX if j == 5 else low + d >= 8)
                    def _():
                        ring(g, j, a, True).start()

    def term(g, j, a):
        d = 1 << (j - 1)
        if j in (4, 6):
            dest = c - d
        elif j == 5:
            dest = c - 8
        else:
            dest = jnp.where(low >= d, c - d, c - d + 8)
        return pltpu.make_async_remote_copy(
            gsend.at[g, j, a], grecv.at[g, j, a], gr_ss.at[g, j, a], gr_rs.at[g, j, a],
            device_id={"ctx": dest}, device_id_type=MESH,
        )

    for a in range(2):
        for o in (1, 3, 2):
            kv_copy(0, a, o).start()

    def send_in(k, _):
        for a in range(2):
            for o in (1, 3, 2):
                in_copy(k, a, o).start()
        return 0

    lax.fori_loop(0, NCH // 2, send_in, 0)
    for o in (1, 3, 2):
        for a in range(2):
            kv_copy(1, a, o).start()
    lax.fori_loop(NCH // 2, NCH, send_in, 0)
    for cp in local[2:]:
        cp.wait()
    send_own(0)
    forward(0)
    for cp in local[:2]:
        cp.wait()

    def relay(g):
        pick = [(5, jnp.logical_and(c >= 8, c + 8 < NCTX))]
        for j in (1, 2, 3):
            pick.append((j, jnp.logical_and(c >= 8, low + (1 << (j - 1)) >= 8)))
        for a in range(2):
            for j, cond in pick:
                @pl.when(cond)
                def _():
                    term(g, j, a).wait_recv()
                    part8[g, a] = part8[g, a] + grecv[g, j, a].astype(F32)
            gsend[g, 4, a] = part8[g, a].astype(BF)

            @pl.when(c >= 8)
            def _():
                term(g, 4, a).start()

    def finish(g):
        pick = [(6, c + 32 < NCTX)]
        for j in (1, 2, 3):
            pick.append((j, low + (1 << (j - 1)) < 8))
        pick.append((4, c + 8 < NCTX))
        for a in range(2):
            for j, cond in pick:
                @pl.when(cond)
                def _():
                    term(g, j, a).wait_recv()
                    own[g, a] = own[g, a] + grecv[g, j, a].astype(F32)
            gfin[g, a] = own[g, a].astype(BF)
            for o in (1, 3, 2):
                fin_copy(g, a, o).start()
            fin_local(g, a).start()

    def group(g, _):
        for j in (1, 2, 3, 5, 6):
            @pl.when(valid[j])
            def _():
                for a in range(2):
                    ring(g, j, a, False).wait_recv()
        for j in range(NL):
            ktb[g, j] = kvb[g, j, 0].T
            vtb[g, j] = kvb[g, j, 1].T

        def body(r, _):
            k = g * (QPK // CH) + r // CH

            @pl.when(lax.rem(r, CH) == 0)
            def _():
                for a in range(2):
                    for o in range(1, NKV):
                        in_copy(k, a, o).wait_recv()

            head(g, r, valid, qbuf, gbuf, kvb, vtb, outb, s_scr, p_scr, ds_scr, gs_scr, qs_scr, st)

            @pl.when(lax.rem(r, CH) == CH - 1)
            def _():
                for o in (1, 3, 2):
                    out_copy(k, 0, o).start()
                out_local(k, 0).start()

            @pl.when(jnp.logical_and(g == 0, r == 1))
            def _():
                send_own(1)

            @pl.when(jnp.logical_and(g == 0, r == 4))
            def _():
                forward(1)

            @pl.when(jnp.logical_and(g == 1, r == 1))
            def _():
                relay(0)

            @pl.when(jnp.logical_and(g == 1, r == 4))
            def _():
                finish(0)

            return 0

        lax.fori_loop(0, QPK, body, 0)
        for a, big, small in ((0, ds_scr, qs_scr), (1, p_scr, gs_scr)):
            for j in (5, 3, 2, 1, 6, 4, 0):
                part = nn(big[j], small[...])
                if j in (0, 4):
                    acc = own if j == 0 else part8
                    acc[g, a] = part
                else:
                    gsend[g, j, a] = part.astype(BF)

                    @pl.when(valid[j])
                    def _():
                        term(g, j, a).start()

        def last(r, _):
            query_grad(g, r, ktb, gqb, ds_scr, st)
            k = g * (QPK // CH) + r // CH

            @pl.when(lax.rem(r, CH) == CH - 1)
            def _():
                for o in (1, 3, 2):
                    out_copy(k, 1, o).start()
                out_local(k, 1).start()

            return 0

        lax.fori_loop(0, QPK, last, 0)
        return 0

    lax.fori_loop(0, GRP, group, 0)
    relay(1)
    finish(1)

    def drain(k, _):
        for a in range(2):
            for o in range(1, NKV):
                in_copy(k, a, o).wait_send()
                out_copy(k, a, o).wait()
            out_local(k, a).wait()
        return 0

    lax.fori_loop(0, NCH, drain, 0)
    for g in range(GRP):
        for a in range(2):
            for o in range(1, NKV):
                kv_copy(g, a, o).wait_send()
                fin_copy(g, a, o).wait()
            fin_local(g, a).wait()
        for j in range(1, NL):
            d = 1 << (j - 1)
            if j in (4, 6):
                cond = c + d < NCTX
            elif j == 5:
                cond = jnp.logical_and(c >= 8, c + 8 < NCTX)
            else:
                cond = jnp.logical_or(low + d < 8, c >= 8)

            @pl.when(cond)
            def _():
                for a in range(2):
                    ring(g, j, a, False).wait_send()

            @pl.when(valid[j])
            def _():
                for a in range(2):
                    term(g, j, a).wait_send()


def settle(*refs):
    n = 4
    src, dst, buf = refs[:n], refs[n : 2 * n], refs[2 * n : 3 * n]
    in_sem, out_sem = refs[3 * n :]
    rows = TOK // NSP
    moves = [(i, pl.ds(k * rows, rows), k) for k in range(NSP) for i in range(n)]
    for i, part, k in moves:
        pltpu.make_async_copy(src[i].at[part], buf[i].at[part], in_sem.at[i, k]).start()
    for i, part, k in moves:
        pltpu.make_async_copy(src[i].at[part], buf[i].at[part], in_sem.at[i, k]).wait()
        pltpu.make_async_copy(buf[i].at[part], dst[i].at[part], out_sem.at[i, k]).start()
    for i, part, k in moves:
        pltpu.make_async_copy(buf[i].at[part], dst[i].at[part], out_sem.at[i, k]).wait()


def shards(query_act, key_act, value_act, grad_out):
    hbm = pl.BlockSpec(memory_space=pl.ANY)
    dma = pltpu.SemaphoreType.DMA
    res = tuple(
        pl.pallas_call(
            kernel,
            out_shape=tuple(jax.ShapeDtypeStruct(a.shape, BF) for a in (query_act, query_act, key_act, value_act)),
            in_specs=[hbm] * 4,
            out_specs=(hbm,) * 4,
            scratch_shapes=[pltpu.VMEM((BLK, QW), BF)] * 2
            + [pltpu.VMEM((GRP, NL, 2, BLK, HD), BF)]
            + [pltpu.VMEM((GRP, NL, HD, BLK), BF)] * 2
            + [pltpu.VMEM((BLK, QW), BF)] * 2
            + [pltpu.VMEM((NL, BLK, BLK), F32)]
            + [pltpu.VMEM((NL, BLK, QPK * BLK), BF)] * 2
            + [pltpu.VMEM((QPK * BLK, HD), BF)] * 2
            + [pltpu.VMEM((QPK, BLK), F32)]
            + [pltpu.VMEM((GRP, NL, 2, BLK, HD), BF)] * 2
            + [pltpu.VMEM((GRP, 2, BLK, HD), F32)] * 2
            + [pltpu.VMEM((GRP, 2, BLK, HD), BF)]
            + [dma((6,))]
            + [dma((NCH, 2, 3))] * 2
            + [dma((GRP, 2, 3))] * 2
            + [dma((GRP, NL, 2))] * 4
            + [dma((NCH, 2, 3))] * 2
            + [dma((NCH, 2))]
            + [dma((GRP, 2, 3))] * 2
            + [dma((GRP, 2))],
            compiler_params=pltpu.CompilerParams(
                vmem_limit_bytes=60 * 2**20, collective_id=0, has_side_effects=True,
            ),
        )(query_act, key_act, value_act, grad_out)
    )
    return tuple(
        pl.pallas_call(
            settle,
            out_shape=tuple(jax.ShapeDtypeStruct(a.shape, BF) for a in res),
            in_specs=[hbm] * 4,
            out_specs=(hbm,) * 4,
            scratch_shapes=[pltpu.VMEM(a.shape, BF) for a in res] + [dma((4, NSP))] * 2,
            compiler_params=pltpu.CompilerParams(vmem_limit_bytes=60 * 2**20),
        )(*res)
    )


def solution(mesh):
    spec = P(("ctx", "kvh"), None)
    return jax.shard_map(shards, mesh=mesh, in_specs=(spec,) * 4, out_specs=(spec,) * 4, check_vma=False)
```

```python
import jax
import jax.numpy as jnp
from jax import lax
from jax.experimental import pallas as pl
from jax.experimental.pallas import tpu as pltpu
from jax.sharding import PartitionSpec as P

HD = 128
QPK = 8
BLK = 256
NL = 7
GRP = 2
NKV = 4
NCTX = 64
TOK = BLK // NKV
CH = 4
NSP = 4
NCH = GRP * QPK // CH
CW = CH * HD
QW = GRP * QPK * HD
KW = GRP * HD
SCALE = HD**-0.5
C2 = SCALE * 1.4426950408889634
F32 = jnp.float32
BF = jnp.bfloat16
MESH = pl.DeviceIdType.MESH
ctx_offsets = (1, 2, 4, 6, 7, 8, 16, 32, 48, 56, 57, 58, 60, 62, 63)


def nt(a, b):
    return lax.dot_general(a, b, (((1,), (1,)), ((), ())), preferred_element_type=F32)


def nn(a, b):
    return lax.dot_general(a, b, (((1,), (0,)), ((), ())), preferred_element_type=F32)


def head(g, r, valid, qbuf, gbuf, kvb, vtb, outb, s_scr, p_scr, ds_scr, gs_scr, qs_scr, st):
    col = pl.multiple_of((g * QPK + r) * HD, HD)
    row = pl.multiple_of(r * BLK, BLK)
    q = qbuf[:, pl.ds(col, HD)]
    go = gbuf[:, pl.ds(col, HD)]
    top = None
    for j in range(NL):
        s = nt(kvb[g, j, 0], q)
        if j == 0:
            u = lax.broadcasted_iota(jnp.int32, (BLK, BLK), 0)
            t = lax.broadcasted_iota(jnp.int32, (BLK, BLK), 1)
            s = jnp.where(u <= t, s, -1e30)
        s_scr[j] = s
        mj = jnp.max(s.reshape(BLK // 8, 8, BLK), axis=0)
        top = mj if j == 0 else jnp.maximum(top, jnp.where(valid[j], mj, -1e30))
    top = jnp.max(top, axis=0, keepdims=True)
    total = jnp.zeros((8, BLK), F32)
    acc = jnp.zeros((HD, BLK), F32)
    for j in range(NL):
        sub = top if j == 0 else jnp.where(valid[j], top, 1e30)
        p = jnp.exp2((s_scr[j] - sub) * C2)
        total = total + jnp.sum(p.reshape(BLK // 8, 8, BLK), axis=0)
        pb = p.astype(BF)
        p_scr[j, :, pl.ds(row, BLK)] = pb
        acc = acc + nn(vtb[g, j], pb)
    inv = 1.0 / jnp.sum(total, axis=0, keepdims=True)
    ot = (acc * inv).astype(BF)
    outb[:, pl.ds(col, HD)] = ot.T
    delta = jnp.sum(ot.astype(F32) * go.T.astype(F32), axis=0, keepdims=True)
    for j in range(NL):
        dp = nt(kvb[g, j, 1], go) - delta
        ds = (p_scr[j, :, pl.ds(row, BLK)].astype(F32) * dp).astype(BF)
        ds_scr[j, :, pl.ds(row, BLK)] = ds
    st[pl.ds(r, 1)] = inv * SCALE
    invb = jnp.broadcast_to(inv, (HD, BLK)).T
    gs_scr[pl.ds(row, BLK), :] = (go.astype(F32) * invb).astype(BF)
    qs_scr[pl.ds(row, BLK), :] = (q.astype(F32) * (invb * SCALE)).astype(BF)


def query_grad(g, r, ktb, gqb, ds_scr, st):
    col = pl.multiple_of((g * QPK + r) * HD, HD)
    row = pl.multiple_of(r * BLK, BLK)
    acc = jnp.zeros((HD, BLK), F32)
    for j in range(NL):
        acc = acc + nn(ktb[g, j], ds_scr[j, :, pl.ds(row, BLK)])
    gqb[:, pl.ds(col, HD)] = (acc * st[pl.ds(r, 1)]).astype(BF).T


def kernel(
    q_in, k_in, v_in, g_in,
    out_o, gq_o, gk_o, gv_o,
    qbuf, gbuf, kvb, ktb, vtb, outb, gqb,
    s_scr, p_scr, ds_scr, gs_scr, qs_scr, st,
    gsend, grecv, own, part8, gfin,
    loc_sem, in_ss, in_rs, kv_ss, kv_rs, ring_ss, ring_rs, gr_ss, gr_rs, out_ss, out_rs, out_loc, fin_ss, fin_rs, fin_loc,
):
    c = lax.axis_index("ctx")
    h = lax.axis_index("kvh")
    low = lax.rem(c, 8)
    valid = [None] + [c >= 1 << j for j in range(NL - 1)]
    mine = pl.ds(pl.multiple_of(h * TOK, TOK), TOK)

    local = [
        pltpu.make_async_copy(q_in.at[:, pl.ds(pl.multiple_of(h * QW, QW), QW)], qbuf.at[mine], loc_sem.at[0]),
        pltpu.make_async_copy(g_in.at[:, pl.ds(pl.multiple_of(h * QW, QW), QW)], gbuf.at[mine], loc_sem.at[1]),
    ]
    for g in range(GRP):
        src = pl.ds(pl.multiple_of(h * KW + g * HD, HD), HD)
        local.append(pltpu.make_async_copy(k_in.at[:, src], kvb.at[g, 0, 0, mine], loc_sem.at[2 + 2 * g]))
        local.append(pltpu.make_async_copy(v_in.at[:, src], kvb.at[g, 0, 1, mine], loc_sem.at[3 + 2 * g]))
    for cp in local:
        cp.start()
    for j in range(1, NL):
        @pl.when(jnp.logical_not(valid[j]))
        def _():
            for g in range(GRP):
                kvb[g, j] = jnp.zeros((2, BLK, HD), BF)

    bar = pltpu.get_barrier_semaphore()
    for o in range(1, NKV):
        pl.semaphore_signal(bar, 1, device_id={"kvh": lax.rem(h + o, NKV)}, device_id_type=MESH)
    for o in ctx_offsets:
        pl.semaphore_signal(bar, 1, device_id={"ctx": lax.rem(c + o, NCTX)}, device_id_type=MESH)
    pl.semaphore_wait(bar, NKV - 1 + len(ctx_offsets))

    def kv_copy(g, a, o):
        p = lax.rem(h + o, NKV)
        ref = (k_in, v_in)[a]
        return pltpu.make_async_remote_copy(
            ref.at[:, pl.ds(pl.multiple_of(p * KW + g * HD, HD), HD)],
            kvb.at[g, 0, a, mine],
            kv_ss.at[g, a, o - 1], kv_rs.at[g, a, o - 1],
            device_id={"kvh": p}, device_id_type=MESH,
        )

    def in_copy(k, a, o):
        p = lax.rem(h + o, NKV)
        ref, buf = ((q_in, qbuf), (g_in, gbuf))[a]
        return pltpu.make_async_remote_copy(
            ref.at[:, pl.ds(pl.multiple_of(p * QW + k * CW, CW), CW)],
            buf.at[mine, pl.ds(pl.multiple_of(k * CW, CW), CW)],
            in_ss.at[k, a, o - 1], in_rs.at[k, a, o - 1],
            device_id={"kvh": p}, device_id_type=MESH,
        )

    def out_copy(k, a, o):
        p = lax.rem(h + o, NKV)
        buf, ref = ((outb, out_o), (gqb, gq_o))[a]
        return pltpu.make_async_remote_copy(
            buf.at[pl.ds(pl.multiple_of(p * TOK, TOK), TOK), pl.ds(pl.multiple_of(k * CW, CW), CW)],
            ref.at[:, pl.ds(pl.multiple_of(h * QW + k * CW, CW), CW)],
            out_ss.at[k, a, o - 1], out_rs.at[k, a, o - 1],
            device_id={"kvh": p}, device_id_type=MESH,
        )

    def out_local(k, a):
        buf, ref = ((outb, out_o), (gqb, gq_o))[a]
        return pltpu.make_async_copy(
            buf.at[mine, pl.ds(pl.multiple_of(k * CW, CW), CW)],
            ref.at[:, pl.ds(pl.multiple_of(h * QW + k * CW, CW), CW)],
            out_loc.at[k, a],
        )

    def fin_copy(g, a, o):
        p = lax.rem(h + o, NKV)
        return pltpu.make_async_remote_copy(
            gfin.at[g, a, pl.ds(pl.multiple_of(p * TOK, TOK), TOK)],
            (gk_o, gv_o)[a].at[:, pl.ds(pl.multiple_of(h * KW + g * HD, HD), HD)],
            fin_ss.at[g, a, o - 1], fin_rs.at[g, a, o - 1],
            device_id={"kvh": p}, device_id_type=MESH,
        )

    def fin_local(g, a):
        return pltpu.make_async_copy(
            gfin.at[g, a, mine],
            (gk_o, gv_o)[a].at[:, pl.ds(pl.multiple_of(h * KW + g * HD, HD), HD)],
            fin_loc.at[g, a],
        )

    def ring(g, j, a, from8):
        src, at = (4, c - 8) if from8 else (0, c)
        return pltpu.make_async_remote_copy(
            kvb.at[g, src, a], kvb.at[g, j, a], ring_ss.at[g, j, a], ring_rs.at[g, j, a],
            device_id={"ctx": at + (1 << (j - 1))}, device_id_type=MESH,
        )

    def send_own(g):
        for a in range(2):
            for o in (1, 3, 2):
                kv_copy(g, a, o).wait_recv()
            for j in (4, 2, 6, 3, 1):
                d = 1 << (j - 1)

                @pl.when(c + d < NCTX if j >= 4 else low + d < 8)
                def _():
                    ring(g, j, a, False).start()

    def forward(g):
        @pl.when(c >= 8)
        def _():
            for a in range(2):
                ring(g, 4, a, False).wait_recv()
                for j in (5, 2, 3, 1):
                    d = 1 << (j - 1)

                    @pl.when(c + 8 < NCTX if j == 5 else low + d >= 8)
                    def _():
                        ring(g, j, a, True).start()

    def term(g, j, a):
        d = 1 << (j - 1)
        if j in (4, 6):
            dest = c - d
        elif j == 5:
            dest = c - 8
        else:
            dest = jnp.where(low >= d, c - d, c - d + 8)
        return pltpu.make_async_remote_copy(
            gsend.at[g, j, a], grecv.at[g, j, a], gr_ss.at[g, j, a], gr_rs.at[g, j, a],
            device_id={"ctx": dest}, device_id_type=MESH,
        )

    for a in range(2):
        for o in (1, 3, 2):
            kv_copy(0, a, o).start()

    def send_in(k, _):
        for a in range(2):
            for o in (1, 3, 2):
                in_copy(k, a, o).start()
        return 0

    lax.fori_loop(0, NCH // 2, send_in, 0)
    for o in (1, 3, 2):
        for a in range(2):
            kv_copy(1, a, o).start()
    lax.fori_loop(NCH // 2, NCH, send_in, 0)
    for cp in local[2:]:
        cp.wait()
    send_own(0)
    forward(0)
    for cp in local[:2]:
        cp.wait()

    def relay(g):
        pick = [(5, jnp.logical_and(c >= 8, c + 8 < NCTX))]
        for j in (1, 2, 3):
            pick.append((j, jnp.logical_and(c >= 8, low + (1 << (j - 1)) >= 8)))
        for a in range(2):
            for j, cond in pick:
                @pl.when(cond)
                def _():
                    term(g, j, a).wait_recv()
                    part8[g, a] = part8[g, a] + grecv[g, j, a].astype(F32)
            gsend[g, 4, a] = part8[g, a].astype(BF)

            @pl.when(c >= 8)
            def _():
                term(g, 4, a).start()

    def finish(g):
        pick = [(6, c + 32 < NCTX)]
        for j in (1, 2, 3):
            pick.append((j, low + (1 << (j - 1)) < 8))
        pick.append((4, c + 8 < NCTX))
        for a in range(2):
            for j, cond in pick:
                @pl.when(cond)
                def _():
                    term(g, j, a).wait_recv()
                    own[g, a] = own[g, a] + grecv[g, j, a].astype(F32)
            gfin[g, a] = own[g, a].astype(BF)
            for o in (1, 3, 2):
                fin_copy(g, a, o).start()
            fin_local(g, a).start()

    def group(g, _):
        for j in (1, 2, 3, 5, 6):
            @pl.when(valid[j])
            def _():
                for a in range(2):
                    ring(g, j, a, False).wait_recv()
        for j in range(NL):
            ktb[g, j] = kvb[g, j, 0].T
            vtb[g, j] = kvb[g, j, 1].T

        def body(r, _):
            k = g * (QPK // CH) + r // CH

            @pl.when(lax.rem(r, CH) == 0)
            def _():
                for a in range(2):
                    for o in range(1, NKV):
                        in_copy(k, a, o).wait_recv()

            head(g, r, valid, qbuf, gbuf, kvb, vtb, outb, s_scr, p_scr, ds_scr, gs_scr, qs_scr, st)

            @pl.when(lax.rem(r, CH) == CH - 1)
            def _():
                for o in (1, 3, 2):
                    out_copy(k, 0, o).start()
                out_local(k, 0).start()

            @pl.when(jnp.logical_and(g == 0, r == 1))
            def _():
                send_own(1)

            @pl.when(jnp.logical_and(g == 0, r == 4))
            def _():
                forward(1)

            @pl.when(jnp.logical_and(g == 1, r == 3))
            def _():
                relay(0)

            @pl.when(jnp.logical_and(g == 1, r == 6))
            def _():
                finish(0)

            return 0

        lax.fori_loop(0, QPK, body, 0)
        for a, big, small in ((0, ds_scr, qs_scr), (1, p_scr, gs_scr)):
            for j in (5, 3, 2, 1, 6, 4, 0):
                part = nn(big[j], small[...])
                if j in (0, 4):
                    acc = own if j == 0 else part8
                    acc[g, a] = part
                else:
                    gsend[g, j, a] = part.astype(BF)

                    @pl.when(valid[j])
                    def _():
                        term(g, j, a).start()

        def last(r, _):
            query_grad(g, r, ktb, gqb, ds_scr, st)
            k = g * (QPK // CH) + r // CH

            @pl.when(lax.rem(r, CH) == CH - 1)
            def _():
                for o in (1, 3, 2):
                    out_copy(k, 1, o).start()
                out_local(k, 1).start()

            return 0

        lax.fori_loop(0, QPK, last, 0)
        return 0

    lax.fori_loop(0, GRP, group, 0)
    relay(1)
    finish(1)

    def drain(k, _):
        for a in range(2):
            for o in range(1, NKV):
                in_copy(k, a, o).wait_send()
                out_copy(k, a, o).wait()
            out_local(k, a).wait()
        return 0

    lax.fori_loop(0, NCH, drain, 0)
    for g in range(GRP):
        for a in range(2):
            for o in range(1, NKV):
                kv_copy(g, a, o).wait_send()
                fin_copy(g, a, o).wait()
            fin_local(g, a).wait()
        for j in range(1, NL):
            d = 1 << (j - 1)
            if j in (4, 6):
                cond = c + d < NCTX
            elif j == 5:
                cond = jnp.logical_and(c >= 8, c + 8 < NCTX)
            else:
                cond = jnp.logical_or(low + d < 8, c >= 8)

            @pl.when(cond)
            def _():
                for a in range(2):
                    ring(g, j, a, False).wait_send()

            @pl.when(valid[j])
            def _():
                for a in range(2):
                    term(g, j, a).wait_send()


def settle(*refs):
    n = 4
    src, dst, buf = refs[:n], refs[n : 2 * n], refs[2 * n : 3 * n]
    in_sem, out_sem = refs[3 * n :]
    rows = TOK // NSP
    moves = [(i, pl.ds(k * rows, rows), k) for k in range(NSP) for i in range(n)]
    for i, part, k in moves:
        pltpu.make_async_copy(src[i].at[part], buf[i].at[part], in_sem.at[i, k]).start()
    for i, part, k in moves:
        pltpu.make_async_copy(src[i].at[part], buf[i].at[part], in_sem.at[i, k]).wait()
        pltpu.make_async_copy(buf[i].at[part], dst[i].at[part], out_sem.at[i, k]).start()
    for i, part, k in moves:
        pltpu.make_async_copy(buf[i].at[part], dst[i].at[part], out_sem.at[i, k]).wait()


def shards(query_act, key_act, value_act, grad_out):
    hbm = pl.BlockSpec(memory_space=pl.ANY)
    dma = pltpu.SemaphoreType.DMA
    res = tuple(
        pl.pallas_call(
            kernel,
            out_shape=tuple(jax.ShapeDtypeStruct(a.shape, BF) for a in (query_act, query_act, key_act, value_act)),
            in_specs=[hbm] * 4,
            out_specs=(hbm,) * 4,
            scratch_shapes=[pltpu.VMEM((BLK, QW), BF)] * 2
            + [pltpu.VMEM((GRP, NL, 2, BLK, HD), BF)]
            + [pltpu.VMEM((GRP, NL, HD, BLK), BF)] * 2
            + [pltpu.VMEM((BLK, QW), BF)] * 2
            + [pltpu.VMEM((NL, BLK, BLK), F32)]
            + [pltpu.VMEM((NL, BLK, QPK * BLK), BF)] * 2
            + [pltpu.VMEM((QPK * BLK, HD), BF)] * 2
            + [pltpu.VMEM((QPK, BLK), F32)]
            + [pltpu.VMEM((GRP, NL, 2, BLK, HD), BF)] * 2
            + [pltpu.VMEM((GRP, 2, BLK, HD), F32)] * 2
            + [pltpu.VMEM((GRP, 2, BLK, HD), BF)]
            + [dma((6,))]
            + [dma((NCH, 2, 3))] * 2
            + [dma((GRP, 2, 3))] * 2
            + [dma((GRP, NL, 2))] * 4
            + [dma((NCH, 2, 3))] * 2
            + [dma((NCH, 2))]
            + [dma((GRP, 2, 3))] * 2
            + [dma((GRP, 2))],
            compiler_params=pltpu.CompilerParams(
                vmem_limit_bytes=60 * 2**20, collective_id=0, has_side_effects=True,
            ),
        )(query_act, key_act, value_act, grad_out)
    )
    return tuple(
        pl.pallas_call(
            settle,
            out_shape=tuple(jax.ShapeDtypeStruct(a.shape, BF) for a in res),
            in_specs=[hbm] * 4,
            out_specs=(hbm,) * 4,
            scratch_shapes=[pltpu.VMEM(a.shape, BF) for a in res] + [dma((4, NSP))] * 2,
            compiler_params=pltpu.CompilerParams(vmem_limit_bytes=60 * 2**20),
        )(*res)
    )


def solution(mesh):
    spec = P(("ctx", "kvh"), None)
    return jax.shard_map(shards, mesh=mesh, in_specs=(spec,) * 4, out_specs=(spec,) * 4, check_vma=False)
```
